32 devices in a mesh: clips: 2 (over x), frames: 2 (over core), rows: 8 (over z, y).
Axes of the slice: x: 2, y: 2, z: 4, core: 2. Of those that a mesh axis runs over, the one named last changes fastest.
Arguments:
- noisy_video: bfloat16 [4, 64, 1024, 128], P(('clips', 'frames'), 'rows'), parts along dimension 0, may hold values from -60 to 60
- timestep: int32 [2], P('clips'), parts along dimension 0, may hold values from 100 to 899
- embed_weight: bfloat16 [512, 256], replicated, may hold values from -0.25 to 0.25
- norm_gain: float32 [2, 128], replicated, may hold values from 0.1 to 1.9
- norm_bias: float32 [2, 128], replicated, may hold values from -2.4 to 2.4
- conv_first: bfloat16 [3, 3, 128, 128], replicated, may hold values from -0.1875 to 0.1875
- temporal_weight: bfloat16 [3, 128, 128], replicated, may hold values from -0.3125 to 0.3125
- conv_second: bfloat16 [3, 3, 128, 128], replicated, may hold values from -0.1875 to 0.1875
Outputs:
- next_video: bfloat16 [4, 64, 1024, 128], P(('clips', 'frames'), 'rows'), parts along dimension 0
- predicted: float32 [4, 64, 1024, 128], P(('clips', 'frames'), 'rows'), parts along dimension 0
The draws below stay inside these ranges and needn't reach their ends.
There are 2 independent parts, one for each index of `clips`. The reference program is written for one: setup_inputs(seed, part) draws one part's arguments, and reference() takes and returns one part's arrays. A program takes and returns all parts, laid end to end along the dimension named above; an argument that names none is the same for every part. Nothing has to cross between parts.
All inputs are finite; a program needn't handle non-finite values.
Results may differ from the reference program's by a relative error of at most 0.002.
Values may be sent and summed in bfloat16 or wider, within the bound.
No kernel may reach another device: no remote copies, remote signals or barrier semaphores. Data moves between devices by JAX's collectives and lax.ppermute only.
A program may use at most 128 MiB of HBM per device.

```python
import math
import jax
import jax.numpy as jnp
from jax import lax

CHANNELS = 128
GROUPS = 32
EMBED = 512
WIDTH_CELLS = 1024
TSTEPS = 1000
STRIDE = 8
FRAMES = 2
HEIGHT = 64


def draw_noisy_video(key, part):
    subkeys = jax.random.split(key, 3)
    full_shape = (FRAMES, HEIGHT, WIDTH_CELLS, CHANNELS)
    row_pos = jnp.arange(HEIGHT, dtype=jnp.float32)
    row_rise = 3.0 ** (row_pos / HEIGHT - 0.5)
    row_scale = jnp.exp(jax.random.uniform(subkeys[1], (HEIGHT,), jnp.float32, math.log(0.6), math.log(1.7)))
    col_scale = jnp.exp(jax.random.uniform(subkeys[2], (WIDTH_CELLS,), jnp.float32, math.log(0.3), math.log(3.0)))
    sample_base = jax.random.normal(subkeys[0], full_shape, jnp.float32)
    cell_scale = (row_rise * row_scale)[None, :, None, None] * col_scale[None, None, :, None]
    return (sample_base * cell_scale).astype(jnp.bfloat16)


def bell_draw(rng, dims, scale, reach, kind=jnp.bfloat16):
    result = jax.random.normal(rng, dims, jnp.float32) * scale
    return jnp.minimum(jnp.maximum(result, -reach), reach).astype(kind)


def setup_inputs(seed: int = 0, part: int = 0) -> dict:
    arg_keys = jax.random.split(jax.random.key(seed), 9)
    part_keys = jax.random.split(jax.random.fold_in(arg_keys[8], part), 9)
    return {
        "noisy_video": draw_noisy_video(jax.random.fold_in(jax.random.fold_in(arg_keys[8], part), 71), part),
        "timestep": jax.random.randint(part_keys[1], (1,), 100, 900).astype(jnp.int32),
        "embed_weight": bell_draw(arg_keys[2], (EMBED, 2 * CHANNELS), EMBED ** -0.5, 0.25),
        "norm_gain": jnp.clip(1.0 + 0.18 * jax.random.normal(arg_keys[3], (2, CHANNELS), jnp.float32), 0.1, 1.9),
        "norm_bias": bell_draw(arg_keys[4], (2, CHANNELS), 0.4, 2.4, jnp.float32),
        "conv_first": bell_draw(arg_keys[5], (3, 3, CHANNELS, CHANNELS), (9 * CHANNELS) ** -0.5, 0.1875),
        "temporal_weight": bell_draw(arg_keys[6], (3, CHANNELS, CHANNELS), (3 * CHANNELS) ** -0.5, 0.3125),
        "conv_second": bell_draw(arg_keys[7], (3, 3, CHANNELS, CHANNELS), (9 * CHANNELS) ** -0.5, 0.1875),
    }


def signal_noise(step_value):
    frac = (step_value.astype(jnp.float32) / TSTEPS + 0.008) / 1.008
    level = jnp.cos(frac * (math.pi / 2)) ** 2
    return (jnp.sqrt(level), jnp.sqrt(1.0 - level))

def embed_time(step_value, embed_weight):
    half = embed_weight.shape[0] // 2
    freqs = jnp.exp(-math.log(10000.0) * jnp.arange(half, dtype=jnp.float32) / half)
    angles = step_value.astype(jnp.float32) * freqs
    feats = jnp.concatenate([jnp.sin(angles), jnp.cos(angles)]).astype(jnp.bfloat16)
    film = jnp.dot(feats[None, :], embed_weight, preferred_element_type=jnp.float32)[0]
    channels = embed_weight.shape[1] // 2
    return (film[:channels], film[channels:])

def group_norm(values, gain, bias):
    frames, height, width, channels = values.shape
    grouped = values.reshape(frames, height, width, GROUPS, channels // GROUPS)
    first = lax.optimization_barrier(jnp.sum(grouped, axis=(1, 2, 4)))
    second = lax.optimization_barrier(jnp.sum(grouped * grouped, axis=(1, 2, 4)))
    count = height * width * (channels // GROUPS)
    mean = first / count
    inverse = lax.rsqrt(second / count - mean * mean + 1e-05)
    mean_ch = jnp.repeat(mean, channels // GROUPS, axis=1)[:, None, None, :]
    inv_ch = jnp.repeat(inverse, channels // GROUPS, axis=1)[:, None, None, :]
    return (values - mean_ch) * inv_ch * gain + bias

def spatial_conv(values, kernel):
    frames, height, width, channels = values.shape
    padded = jnp.pad(values, ((0, 0), (1, 1), (1, 1), (0, 0)))
    total = jnp.zeros((frames * height * width, kernel.shape[3]), jnp.float32)
    for offset_row in range(3):
        for offset_col in range(3):
            window = padded[:, offset_row:offset_row + height, offset_col:offset_col + width, :]
            total = total + jnp.dot(window.reshape(-1, channels), kernel[offset_row, offset_col], preferred_element_type=jnp.float32)
    return total.reshape(frames, height, width, kernel.shape[3])

def reference(noisy_video, timestep, embed_weight, norm_gain, norm_bias, conv_first, temporal_weight, conv_second):
    step_now = timestep[0]
    scale, shift = embed_time(step_now, embed_weight)
    signal_now, noise_now = signal_noise(step_now)
    signal_prev, noise_prev = signal_noise(step_now - STRIDE)
    video = noisy_video.astype(jnp.float32)
    activated = jax.nn.silu(group_norm(video, norm_gain[0], norm_bias[0])).astype(jnp.bfloat16)
    first = (spatial_conv(activated, conv_first) * (1.0 + scale) + shift).astype(jnp.bfloat16)
    mixed = jax.nn.silu(group_norm(first.astype(jnp.float32), norm_gain[1], norm_bias[1])).astype(jnp.bfloat16)
    frames, height, width, channels = mixed.shape
    framed = jnp.pad(mixed, ((1, 1), (0, 0), (0, 0), (0, 0)))
    total = jnp.zeros((frames * height * width, channels), jnp.float32)
    for offset in range(3):
        total = total + jnp.dot(framed[offset:offset + frames].reshape(-1, channels), temporal_weight[offset], preferred_element_type=jnp.float32)
    temporal = total.reshape(frames, height, width, channels).astype(jnp.bfloat16)
    predicted = (video + spatial_conv(temporal, conv_second)) * (1.0 / math.sqrt(2.0))
    estimate = (video - noise_now * predicted) / signal_now
    return ((signal_prev * estimate + noise_prev * predicted).astype(jnp.bfloat16), predicted)
```

```python
import functools
import math

import jax
import jax.numpy as jnp
from jax import lax
from jax.experimental import pallas as pl
from jax.experimental.pallas import tpu as pltpu
from jax.sharding import PartitionSpec as P

GROUPS = 32
TSTEPS = 1000
STRIDE = 8
PAD = 8
F32 = jnp.float32
BF16 = jnp.bfloat16
VMEM_LIMIT = 56 * 1024 * 1024


def signal_noise(step_value):
    frac = (step_value.astype(F32) / TSTEPS + 0.008) / 1.008
    level = jnp.cos(frac * (math.pi / 2)) ** 2
    return (jnp.sqrt(level), jnp.sqrt(1.0 - level))


def embed_time(step_value, embed_weight):
    half = embed_weight.shape[0] // 2
    freqs = jnp.exp(-math.log(10000.0) * jnp.arange(half, dtype=F32) / half)
    angles = step_value.astype(F32) * freqs
    feats = jnp.concatenate([jnp.sin(angles), jnp.cos(angles)]).astype(BF16)
    return jnp.dot(feats[None, :], embed_weight, preferred_element_type=F32)


def fold(values):
    return jnp.sum(values.reshape(-1, 8, values.shape[-1]), axis=0)


def moments_kernel(x_ref, out_ref):
    step = pl.program_id(0)

    @pl.when(step == 0)
    def _():
        out_ref[...] = jnp.zeros_like(out_ref)

    values = x_ref[...].reshape(-1, x_ref.shape[-1]).astype(F32)
    out_ref[0:8] += fold(values)
    out_ref[8:16] += fold(values * values)


def moments(x):
    rows, width, channels = x.shape
    return pl.pallas_call(
        moments_kernel,
        grid=(rows // 2,),
        in_specs=[pl.BlockSpec((2, width, channels), lambda i: (i, 0, 0))],
        out_specs=pl.BlockSpec((16, channels), lambda i: (0, 0)),
        out_shape=jax.ShapeDtypeStruct((16, channels), F32),
        name="moments",
    )(x)


def half_factors(sums, gain, bias, count, per_group):
    first = jnp.sum(sums[0:8], axis=0, keepdims=True)
    second = jnp.sum(sums[8:16], axis=0, keepdims=True)
    both = jnp.concatenate([first, second] * 4, axis=0)
    channels = both.shape[1]
    lane = lax.broadcasted_iota(jnp.int32, both.shape, 1)
    total, reach = both, 1
    while reach < per_group:
        up = pltpu.roll(total, channels - reach, 1)
        down = pltpu.roll(total, reach, 1)
        total = total + jnp.where((lane // reach) % 2 == 0, up, down)
        reach *= 2
    mean = total[0:1] / count
    inverse = lax.rsqrt(total[1:2] / count - mean * mean + 1e-05)
    scale = inverse * gain
    return 0.5 * scale, 0.5 * (bias - mean * scale)


def half_silu(value, scale, offset):
    half = value.astype(F32) * scale + offset
    return half + half * jnp.tanh(half)


def spread(value, pad_ref, taps_ref, at):
    width, channels = value.shape
    pad_ref[PAD : PAD + width] = value
    for tap in range(3):
        low = PAD + tap - 1
        taps_ref[at, :, tap * channels : (tap + 1) * channels] = pad_ref[low : low + width].astype(BF16)


def clear_pads(pad_ref, width):
    for low in (0, PAD + width):
        pad_ref[low : low + PAD] = jnp.zeros((PAD, pad_ref.shape[1]), F32)


def pair_weights(kernel_ref, pair_ref):
    depth, channels = kernel_ref.shape[1:]
    for row in range(4):
        for out in range(2):
            block = pair_ref.at[row * depth : (row + 1) * depth, out * channels : (out + 1) * channels]
            if 0 <= row - out <= 2:
                block[...] = kernel_ref[row - out]
            else:
                block[...] = jnp.zeros((depth, channels), BF16)


def pair_dot(taps_ref, first, pair_ref):
    left = jnp.concatenate([taps_ref[first + row] for row in range(4)], axis=1)
    return jnp.dot(left, pair_ref[...], preferred_element_type=F32)


def conv_one_kernel(
    count, per_group, edge_ref, low_ref, x_low_ref, x_high_ref, high_ref, sums_ref, gain_ref, bias_ref,
    film_ref, kernel_ref, out_ref, stats_ref, pad_a, pad_b, taps_ref, pair_ref, factor_ref,
):
    step = pl.program_id(0)
    last = pl.num_programs(0) - 1
    width, channels = low_ref.shape[1:]

    @pl.when(step == 0)
    def _():
        scale, offset = half_factors(sums_ref[...], gain_ref[...], bias_ref[...], count, per_group)
        factor_ref[0:1] = scale
        factor_ref[1:2] = offset
        clear_pads(pad_a, width)
        clear_pads(pad_b, width)
        pair_weights(kernel_ref, pair_ref)
        stats_ref[...] = jnp.zeros_like(stats_ref)

    scale, offset = factor_ref[0:1], factor_ref[1:2]
    keep_low = jnp.where(step == 0, edge_ref[0], 1).astype(F32)
    keep_high = jnp.where(step == last, edge_ref[1], 1).astype(F32)
    row_low = jnp.where(step == 0, low_ref[0], x_low_ref[0])
    row_high = jnp.where(step == last, high_ref[0], x_high_ref[0])
    spread(half_silu(row_low, scale, offset) * keep_low, pad_a, taps_ref, 2 * step)
    spread(half_silu(row_high, scale, offset) * keep_high, pad_b, taps_ref, 2 * step + 1)

    @pl.when(step > 0)
    def _():
        result = pair_dot(taps_ref, 2 * step - 2, pair_ref)
        gain = 1.0 + film_ref[0:1, :channels]
        shift = film_ref[0:1, channels:]
        for out in range(2):
            value = (result[:, out * channels : (out + 1) * channels] * gain + shift).astype(BF16)
            out_ref[out] = value
            value = value.astype(F32)
            stats_ref[0:8] += fold(value)
            stats_ref[8:16] += fold(value * value)


def whole(*shape):
    return pl.BlockSpec(shape, lambda *_: (0,) * len(shape))


def conv_one(x, low, high, edge, sums, gain, bias, film, kernel, count, per_group):
    rows, width, channels = x.shape
    steps = rows // 2 + 1
    depth = 3 * channels
    row = (1, width, channels)
    return pl.pallas_call(
        functools.partial(conv_one_kernel, count, per_group),
        grid=(steps,),
        in_specs=[
            pl.BlockSpec(memory_space=pltpu.SMEM),
            whole(*row),
            pl.BlockSpec(row, lambda i: (jnp.maximum(2 * i - 1, 0), 0, 0)),
            pl.BlockSpec(row, lambda i: (jnp.minimum(2 * i, rows - 1), 0, 0)),
            whole(*row),
            whole(16, channels),
            whole(1, channels),
            whole(1, channels),
            whole(1, 2 * channels),
            whole(3, depth, channels),
        ],
        out_specs=[
            pl.BlockSpec((2, width, channels), lambda i: (jnp.maximum(i - 1, 0), 0, 0)),
            whole(16, channels),
        ],
        out_shape=[
            jax.ShapeDtypeStruct((rows, width, channels), BF16),
            jax.ShapeDtypeStruct((16, channels), F32),
        ],
        scratch_shapes=[
            pltpu.VMEM((width + 2 * PAD, channels), F32),
            pltpu.VMEM((width + 2 * PAD, channels), F32),
            pltpu.VMEM((rows + 2, width, depth), BF16),
            pltpu.VMEM((4 * depth, 2 * channels), BF16),
            pltpu.VMEM((8, channels), F32),
        ],
        compiler_params=pltpu.CompilerParams(vmem_limit_bytes=VMEM_LIMIT),
        cost_estimate=pl.CostEstimate(flops=18 * rows * width * channels * channels, bytes_accessed=4 * rows * width * channels, transcendentals=rows * width * channels),
        name="conv_one",
    )(edge, low, x, x, high, sums, gain, bias, film, kernel)


def outer_rows_kernel(
    count, per_group, low_a, low_b, x_low, x_high, high_a, high_b, sums_ref, gain_ref, bias_ref,
    film_ref, kernel_ref, out_ref, pad_ref, taps_ref,
):
    step = pl.program_id(0)
    width, channels = low_a.shape[1:]
    scale, offset = half_factors(sums_ref[...], gain_ref[...], bias_ref[...], count, per_group)

    @pl.when(step == 0)
    def _():
        clear_pads(pad_ref, width)

    is_low = step == 0
    for at, (low, high) in enumerate(((low_a, x_high), (low_b, high_a), (x_low, high_b))):
        row = jnp.where(is_low, low[0], high[0])
        spread(half_silu(row, scale, offset), pad_ref, taps_ref, at)
    left = jnp.concatenate([taps_ref[row] for row in range(3)], axis=1)
    weights = kernel_ref[...].reshape(-1, channels)
    result = jnp.dot(left, weights, preferred_element_type=F32)
    out_ref[0] = (result * (1.0 + film_ref[0:1, :channels]) + film_ref[0:1, channels:]).astype(BF16)


def outer_rows(x, low_a, low_b, high_a, high_b, sums, gain, bias, film, kernel, count, per_group):
    rows, width, channels = x.shape
    depth = 3 * channels
    row = (1, width, channels)
    return pl.pallas_call(
        functools.partial(outer_rows_kernel, count, per_group),
        grid=(2,),
        in_specs=[
            whole(*row),
            whole(*row),
            whole(*row),
            pl.BlockSpec(row, lambda i: (rows - 1, 0, 0)),
            whole(*row),
            whole(*row),
            whole(16, channels),
            whole(1, channels),
            whole(1, channels),
            whole(1, 2 * channels),
            whole(3, depth, channels),
        ],
        out_specs=pl.BlockSpec(row, lambda i: (i, 0, 0)),
        out_shape=jax.ShapeDtypeStruct((2, width, channels), BF16),
        scratch_shapes=[
            pltpu.VMEM((width + 2 * PAD, channels), F32),
            pltpu.VMEM((3, width, depth), BF16),
        ],
        compiler_params=pltpu.CompilerParams(vmem_limit_bytes=VMEM_LIMIT),
        cost_estimate=pl.CostEstimate(flops=36 * width * channels * channels, bytes_accessed=12 * width * channels, transcendentals=6 * width * channels),
        name="outer_rows",
    )(low_a, low_b, x, x, high_a, high_b, sums, gain, bias, film, kernel)


def final_kernel(
    count, per_group, edge_ref, plan_ref, mine_ref, mine_low, mine_high, other_ref, other_low, other_high,
    x_ref, sums_ref, other_sums_ref, gain_ref, bias_ref, temporal_ref, kernel_ref,
    next_ref, pred_ref, pad_a, pad_b, taps_ref, pair_ref, factor_ref,
):
    step = pl.program_id(0)
    last = pl.num_programs(0) - 1
    width, channels = mine_low.shape[1:]

    @pl.when(step == 0)
    def _():
        for at, ref in enumerate((sums_ref, other_sums_ref)):
            scale, offset = half_factors(ref[...], gain_ref[...], bias_ref[...], count, per_group)
            factor_ref[2 * at : 2 * at + 1] = scale
            factor_ref[2 * at + 1 : 2 * at + 2] = offset
        clear_pads(pad_a, width)
        clear_pads(pad_b, width)
        pair_weights(kernel_ref, pair_ref)

    keep_low = jnp.where(step == 0, edge_ref[0], 1).astype(F32)
    keep_high = jnp.where(step == last, edge_ref[1], 1).astype(F32)

    def temporal(mine, other, keep):
        a = half_silu(mine, factor_ref[0:1], factor_ref[1:2]).astype(BF16)
        b = half_silu(other, factor_ref[2:3], factor_ref[3:4]).astype(BF16)
        both = jnp.concatenate([a, b], axis=1)
        return jnp.dot(both, temporal_ref[...], preferred_element_type=F32) * keep

    low = temporal(
        jnp.where(step == 0, mine_low[0], mine_ref[0]), jnp.where(step == 0, other_low[0], other_ref[0]), keep_low
    )
    spread(low, pad_a, taps_ref, 2 * step)
    high = temporal(
        jnp.where(step == last, mine_high[0], mine_ref[1]), jnp.where(step == last, other_high[0], other_ref[1]), keep_high
    )
    spread(high, pad_b, taps_ref, 2 * step + 1)

    @pl.when(step > 0)
    def _():
        result = pair_dot(taps_ref, 2 * step - 2, pair_ref)
        for out in range(2):
            video = x_ref[out].astype(F32)
            predicted = (video + result[:, out * channels : (out + 1) * channels]) * (1.0 / math.sqrt(2.0))
            pred_ref[out] = predicted
            next_ref[out] = (plan_ref[0] * video + plan_ref[1] * predicted).astype(BF16)


def body(noisy_video, timestep, embed_weight, norm_gain, norm_bias, conv_first, temporal_weight, conv_second):
    frames, rows, width, channels = noisy_video.shape
    bands = lax.axis_size("rows")
    assert frames == 1 and lax.axis_size("frames") == 2
    assert rows % 2 == 0 and bands & (bands - 1) == 0
    per_group = channels // GROUPS
    count = rows * bands * width * per_group
    x = noisy_video[0]
    band = lax.axis_index("rows")
    frame = lax.axis_index("frames")
    edge = jnp.stack([band > 0, band < bands - 1]).astype(jnp.int32)

    forward = [(i, i + 1) for i in range(bands - 1)]
    backward = [(b, a) for a, b in forward]
    swap = [(0, 1), (1, 0)]

    def all_bands(value):
        reach = 1
        while reach < bands:
            value = value + lax.ppermute(value, "rows", [(i, i ^ reach) for i in range(bands)])
            reach *= 2
        return value

    low_b = lax.ppermute(x[rows - 1 :], "rows", forward)
    high_a = lax.ppermute(x[:1], "rows", backward)
    low_a = lax.ppermute(x[rows - 2 : rows - 1], "rows", forward)
    high_b = lax.ppermute(x[1:2], "rows", backward)

    step_now = timestep[0]
    film = embed_time(step_now, embed_weight)
    signal_now, noise_now = signal_noise(step_now)
    signal_prev, noise_prev = signal_noise(step_now - STRIDE)
    ratio = signal_prev / signal_now
    plan = jnp.stack([ratio, noise_prev - ratio * noise_now])

    sums_one = all_bands(moments(x))
    gain_one, bias_one = norm_gain[0:1], norm_bias[0:1]
    kernel_one = conv_first.reshape(3, 3 * channels, channels)
    first, partial = conv_one(
        x, low_b, high_a, edge, sums_one, gain_one, bias_one, film, kernel_one, count, per_group
    )
    other = lax.ppermute(first, "frames", swap)
    outer = outer_rows(
        x, low_a, low_b, high_a, high_b, sums_one, gain_one, bias_one, film, kernel_one, count, per_group
    )
    other_outer = lax.ppermute(outer, "frames", swap)
    sums_two = all_bands(partial)
    other_two = lax.ppermute(sums_two, "frames", swap)
    side = jnp.where(frame == 0, temporal_weight[2], temporal_weight[0])
    mixing = jnp.concatenate([temporal_weight[1], side], axis=0)

    depth = 3 * channels
    steps = rows // 2 + 1
    row = (1, width, channels)
    next_video, predicted = final(
        edge, plan, first, outer, other, other_outer, x, sums_two, other_two,
        norm_gain[1:2], norm_bias[1:2], mixing, conv_second.reshape(3, depth, channels), count, per_group,
    )
    return next_video[None], predicted[None]


def final(edge, plan, first, outer, other, other_outer, x, sums, other_sums, gain, bias, mixing, kernel, count, per_group):
    rows, width, channels = x.shape
    depth = 3 * channels
    steps = rows // 2 + 1
    row = (1, width, channels)
    low_row = pl.BlockSpec(row, lambda i: (0, 0, 0))
    high_row = pl.BlockSpec(row, lambda i: (1, 0, 0))
    odd = pl.BlockSpec(row, lambda i: (jnp.maximum(2 * i - 1, 0), 0, 0))
    even = pl.BlockSpec(row, lambda i: (jnp.minimum(2 * i, rows - 1), 0, 0))
    pair = pl.BlockSpec((2, width, channels), lambda i: (jnp.maximum(i - 1, 0), 0, 0))

    def kernel_body(edge_ref, plan_ref, m_odd, m_even, m_low, m_high, o_odd, o_even, o_low, o_high, *rest):
        class Rows:
            def __init__(self, a, b):
                self.refs = (a, b)

            def __getitem__(self, at):
                return self.refs[at][0]

        final_kernel(
            count, per_group, edge_ref, plan_ref, Rows(m_odd, m_even), m_low, m_high,
            Rows(o_odd, o_even), o_low, o_high, *rest,
        )

    return pl.pallas_call(
        kernel_body,
        grid=(steps,),
        in_specs=[
            pl.BlockSpec(memory_space=pltpu.SMEM),
            pl.BlockSpec(memory_space=pltpu.SMEM),
            odd, even, low_row, high_row,
            odd, even, low_row, high_row,
            pair,
            whole(16, channels),
            whole(16, channels),
            whole(1, channels),
            whole(1, channels),
            whole(2 * channels, channels),
            whole(3, depth, channels),
        ],
        out_specs=[pair, pair],
        out_shape=[
            jax.ShapeDtypeStruct((rows, width, channels), BF16),
            jax.ShapeDtypeStruct((rows, width, channels), F32),
        ],
        scratch_shapes=[
            pltpu.VMEM((width + 2 * PAD, channels), F32),
            pltpu.VMEM((width + 2 * PAD, channels), F32),
            pltpu.VMEM((rows + 2, width, depth), BF16),
            pltpu.VMEM((4 * depth, 2 * channels), BF16),
            pltpu.VMEM((8, channels), F32),
        ],
        compiler_params=pltpu.CompilerParams(vmem_limit_bytes=VMEM_LIMIT),
        cost_estimate=pl.CostEstimate(flops=24 * rows * width * channels * channels, bytes_accessed=12 * rows * width * channels, transcendentals=2 * rows * width * channels),
        name="final",
    )(edge, plan, first, first, outer, outer, other, other, other_outer, other_outer, x, sums, other_sums, gain, bias, mixing, kernel)


def solution(mesh):
    image = P(("clips", "frames"), "rows", None, None)
    return jax.shard_map(
        body,
        mesh=mesh,
        in_specs=(image, P("clips"), P(), P(), P(), P(), P(), P()),
        out_specs=(image, image),
        check_vma=False,
    )
```

```python
import functools
import math

import jax
import jax.numpy as jnp
from jax import lax
from jax.experimental import pallas as pl
from jax.experimental.pallas import tpu as pltpu
from jax.sharding import PartitionSpec as P

GROUPS = 32
TSTEPS = 1000
STRIDE = 8
PAD = 8
CHUNK = 128
F32 = jnp.float32
BF16 = jnp.bfloat16
VMEM_LIMIT = 56 * 1024 * 1024


def signal_noise(step_value):
    frac = (step_value.astype(F32) / TSTEPS + 0.008) / 1.008
    level = jnp.cos(frac * (math.pi / 2)) ** 2
    return (jnp.sqrt(level), jnp.sqrt(1.0 - level))


def embed_time(step_value, embed_weight):
    half = embed_weight.shape[0] // 2
    freqs = jnp.exp(-math.log(10000.0) * jnp.arange(half, dtype=F32) / half)
    angles = step_value.astype(F32) * freqs
    feats = jnp.concatenate([jnp.sin(angles), jnp.cos(angles)]).astype(BF16)
    return jnp.dot(feats[None, :], embed_weight, preferred_element_type=F32)


def fold(values):
    pixels, channels = values.shape
    wide = jnp.sum(values.reshape(-1, 64, channels), axis=0)
    return jnp.sum(wide.reshape(-1, 8, channels), axis=0)


def moments_kernel(x_ref, out_ref):
    step = pl.program_id(0)

    @pl.when(step == 0)
    def _():
        out_ref[...] = jnp.zeros_like(out_ref)

    rows, width, channels = x_ref.shape
    first = second = None
    for row in range(rows):
        for low in range(0, width, 128):
            values = x_ref[row, low : low + 128].astype(F32).reshape(-1, 32, channels)
            for piece in range(values.shape[0]):
                value = values[piece]
                square = value * value
                first = value if first is None else first + value
                second = square if second is None else second + square
    out_ref[0:8] += jnp.sum(first.reshape(-1, 8, channels), axis=0)
    out_ref[8:16] += jnp.sum(second.reshape(-1, 8, channels), axis=0)


def moments(x):
    rows, width, channels = x.shape
    return pl.pallas_call(
        moments_kernel,
        grid=(rows // 2,),
        in_specs=[pl.BlockSpec((2, width, channels), lambda i: (i, 0, 0))],
        out_specs=pl.BlockSpec((16, channels), lambda i: (0, 0)),
        out_shape=jax.ShapeDtypeStruct((16, channels), F32),
        cost_estimate=pl.CostEstimate(flops=3 * rows * width * channels, bytes_accessed=2 * rows * width * channels, transcendentals=0),
        name="moments",
    )(x)


def half_factors(sums, gain, bias, count, per_group):
    first = jnp.sum(sums[0:8], axis=0, keepdims=True)
    second = jnp.sum(sums[8:16], axis=0, keepdims=True)
    both = jnp.concatenate([first, second] * 4, axis=0)
    channels = both.shape[1]
    lane = lax.broadcasted_iota(jnp.int32, both.shape, 1)
    total, reach = both, 1
    while reach < per_group:
        up = pltpu.roll(total, channels - reach, 1)
        down = pltpu.roll(total, reach, 1)
        total = total + jnp.where((lane // reach) % 2 == 0, up, down)
        reach *= 2
    mean = total[0:1] / count
    inverse = lax.rsqrt(total[1:2] / count - mean * mean + 1e-05)
    scale = inverse * gain
    return 0.5 * scale, 0.5 * (bias - mean * scale)


def half_silu(value, scale, offset):
    half = value.astype(F32) * scale + offset
    return half + half * jnp.tanh(half)


def spread_row(source, width, channels, pad_ref, taps_ref, at):
    for low in range(0, width, CHUNK):
        value = source(low, low + CHUNK)
        pad_ref[PAD + low : PAD + low + CHUNK] = value
        taps_ref[at, low : low + CHUNK, channels : 2 * channels] = value.astype(BF16)
    for low in range(0, width, CHUNK):
        for tap in (0, 2):
            start = PAD + low + tap - 1
            taps_ref[at, low : low + CHUNK, tap * channels : (tap + 1) * channels] = pad_ref[
                start : start + CHUNK
            ].astype(BF16)


def clear_pads(pad_ref, width):
    for low in (0, PAD + width):
        pad_ref[low : low + PAD] = jnp.zeros((PAD, pad_ref.shape[1]), F32)


def pair_weights(kernel_ref, pair_ref):
    depth, channels = kernel_ref.shape[1:]
    for row in range(4):
        for out in range(2):
            block = pair_ref.at[row * depth : (row + 1) * depth, out * channels : (out + 1) * channels]
            if 0 <= row - out <= 2:
                block[...] = kernel_ref[row - out]
            else:
                block[...] = jnp.zeros((depth, channels), BF16)


def pair_dot(taps_ref, first, pair_ref, low, high):
    left = jnp.concatenate([taps_ref[first + row, low:high] for row in range(4)], axis=1)
    return jnp.dot(left, pair_ref[...], preferred_element_type=F32)


def row_copies(low_ref, x_ref, high_ref, ext_ref, sem):
    rows = x_ref.shape[0]
    pairs = [[(low_ref.at[0], 0), (x_ref.at[0], 1)]]
    for pair in range(1, rows // 2):
        pairs.append([(x_ref.at[2 * pair - 1], 2 * pair), (x_ref.at[2 * pair], 2 * pair + 1)])
    pairs.append([(x_ref.at[rows - 1], rows), (high_ref.at[0], rows + 1)])
    return [[pltpu.make_async_copy(ref, ext_ref.at[at], sem.at[at]) for ref, at in pair] for pair in pairs]


def staggered(pairs, ready, fill, drain):
    for step in range(pairs + 1):
        if step < pairs:
            ready(step)
        for part in range(2):
            if step < pairs:
                fill(2 * step + part)
            if step >= 2:
                drain(step - 2, part)


def conv_one_kernel(
    count, per_group, edge_ref, low_ref, x_ref, high_ref, sums_ref, gain_ref, bias_ref,
    film_ref, kernel_ref, out_ref, stats_ref, ext_ref, made_ref, pad_ref, taps_ref, pair_ref, sem, out_sem,
):
    rows, width, channels = x_ref.shape
    copies = row_copies(low_ref, x_ref, high_ref, ext_ref, sem)
    for pair in copies:
        for copy in pair:
            copy.start()
    scale, offset = half_factors(sums_ref[...], gain_ref[...], bias_ref[...], count, per_group)
    gain = 1.0 + film_ref[0:1, :channels]
    shift = film_ref[0:1, channels:]
    for part in range(2):
        clear_pads(pad_ref.at[part], width)
    pair_weights(kernel_ref, pair_ref)
    stats_ref[...] = jnp.zeros_like(stats_ref)
    stores = []

    def ready(pair):
        for copy in copies[pair]:
            copy.wait()

    def fill(at):
        keep = outside(edge_ref, at, rows)

        def activated(low, high):
            value = half_silu(ext_ref[at, low:high], scale, offset)
            return value if keep is None else value * keep

        spread_row(activated, width, channels, pad_ref.at[at % 2], taps_ref, at)

    def drain(pair, part):
        half = width // 2
        low = part * half
        result = pair_dot(taps_ref, 2 * pair, pair_ref, low, low + half)
        first = second = 0.0
        for out in range(2):
            value = result[:, out * channels : (out + 1) * channels] * gain + shift
            made_ref[2 * pair + out, low : low + half] = value.astype(BF16)
            first += fold(value)
            second += fold(value * value)
        stats_ref[0:8] += first
        stats_ref[8:16] += second
        if part == 1:
            band = pl.ds(2 * pair, 2)
            stores.append(pltpu.make_async_copy(made_ref.at[band], out_ref.at[band], out_sem.at[pair]))
            stores[-1].start()

    staggered(rows // 2 + 1, ready, fill, drain)
    for store in stores:
        store.wait()


def outside(edge_ref, at, rows):
    if at == 0:
        return edge_ref[0].astype(F32)
    return edge_ref[1].astype(F32) if at == rows + 1 else None


def whole(*shape):
    return pl.BlockSpec(shape, lambda *_: (0,) * len(shape))


def conv_one(x, low, high, edge, sums, gain, bias, film, kernel, count, per_group):
    rows, width, channels = x.shape
    depth = 3 * channels
    anywhere = pl.BlockSpec(memory_space=pl.ANY)
    return pl.pallas_call(
        functools.partial(conv_one_kernel, count, per_group),
        in_specs=[
            pl.BlockSpec(memory_space=pltpu.SMEM),
            anywhere,
            anywhere,
            anywhere,
            whole(16, channels),
            whole(1, channels),
            whole(1, channels),
            whole(1, 2 * channels),
            whole(3, depth, channels),
        ],
        out_specs=[anywhere, whole(16, channels)],
        out_shape=[
            jax.ShapeDtypeStruct((rows, width, channels), BF16),
            jax.ShapeDtypeStruct((16, channels), F32),
        ],
        scratch_shapes=[
            pltpu.VMEM((rows + 2, width, channels), BF16),
            pltpu.VMEM((rows, width, channels), BF16),
            pltpu.VMEM((2, width + 2 * PAD, channels), F32),
            pltpu.VMEM((rows + 2, width, depth), BF16),
            pltpu.VMEM((4 * depth, 2 * channels), BF16),
            pltpu.SemaphoreType.DMA((rows + 2,)),
            pltpu.SemaphoreType.DMA((rows // 2,)),
        ],
        compiler_params=pltpu.CompilerParams(vmem_limit_bytes=VMEM_LIMIT),
        cost_estimate=pl.CostEstimate(flops=18 * rows * width * channels * channels, bytes_accessed=4 * rows * width * channels, transcendentals=rows * width * channels),
        name="conv_one",
    )(edge, low, x, high, sums, gain, bias, film, kernel)


def outer_rows_kernel(
    count, per_group, low_a, low_b, x_low, x_high, high_a, high_b, sums_ref, gain_ref, bias_ref,
    film_ref, kernel_ref, out_ref, pad_ref, taps_ref,
):
    step = pl.program_id(0)
    width, channels = low_a.shape[1:]
    scale, offset = half_factors(sums_ref[...], gain_ref[...], bias_ref[...], count, per_group)

    for part in range(3):
        clear_pads(pad_ref.at[part], width)
    is_low = step == 0
    for at, (lower, upper) in enumerate(((low_a, x_high), (low_b, high_a), (x_low, high_b))):
        spread_row(
            lambda low, high, a=lower, b=upper: half_silu(
                jnp.where(is_low, a[0, low:high], b[0, low:high]), scale, offset
            ),
            width, channels, pad_ref.at[at], taps_ref, at,
        )
    left = jnp.concatenate([taps_ref[row] for row in range(3)], axis=1)
    weights = kernel_ref[...].reshape(-1, channels)
    result = jnp.dot(left, weights, preferred_element_type=F32)
    out_ref[0] = (result * (1.0 + film_ref[0:1, :channels]) + film_ref[0:1, channels:]).astype(BF16)


def outer_rows(x, low_a, low_b, high_a, high_b, sums, gain, bias, film, kernel, count, per_group):
    rows, width, channels = x.shape
    depth = 3 * channels
    row = (1, width, channels)
    return pl.pallas_call(
        functools.partial(outer_rows_kernel, count, per_group),
        grid=(2,),
        in_specs=[
            whole(*row),
            whole(*row),
            whole(*row),
            pl.BlockSpec(row, lambda i: (rows - 1, 0, 0)),
            whole(*row),
            whole(*row),
            whole(16, channels),
            whole(1, channels),
            whole(1, channels),
            whole(1, 2 * channels),
            whole(3, depth, channels),
        ],
        out_specs=pl.BlockSpec(row, lambda i: (i, 0, 0)),
        out_shape=jax.ShapeDtypeStruct((2, width, channels), BF16),
        scratch_shapes=[
            pltpu.VMEM((3, width + 2 * PAD, channels), F32),
            pltpu.VMEM((3, width, depth), BF16),
        ],
        compiler_params=pltpu.CompilerParams(vmem_limit_bytes=VMEM_LIMIT),
        cost_estimate=pl.CostEstimate(flops=36 * width * channels * channels, bytes_accessed=12 * width * channels, transcendentals=6 * width * channels),
        name="outer_rows",
    )(low_a, low_b, x, x, high_a, high_b, sums, gain, bias, film, kernel)


def final_kernel(
    count, per_group, edge_ref, plan_ref, mine_ref, mine_outer, other_ref, other_outer,
    x_ref, sums_ref, other_sums_ref, gain_ref, bias_ref, temporal_ref, kernel_ref,
    next_ref, pred_ref, mine_ext, other_ext, x_ext, next_made, pred_made, pad_ref, taps_ref, pair_ref,
    mine_sem, other_sem, x_sem, next_sem, pred_sem,
):
    rows, width, channels = mine_ref.shape
    mine_copies = row_copies(mine_outer.at[0:1], mine_ref, mine_outer.at[1:2], mine_ext, mine_sem)
    other_copies = row_copies(other_outer.at[0:1], other_ref, other_outer.at[1:2], other_ext, other_sem)
    copies = [a + b for a, b in zip(mine_copies, other_copies)]
    for pair in copies:
        for copy in pair:
            copy.start()
    x_copies = []
    for pair in range(rows // 2):
        band = pl.ds(2 * pair, 2)
        x_copies.append(pltpu.make_async_copy(x_ref.at[band], x_ext.at[band], x_sem.at[pair]))
        x_copies[-1].start()
    mine_factors = half_factors(sums_ref[...], gain_ref[...], bias_ref[...], count, per_group)
    other_factors = half_factors(other_sums_ref[...], gain_ref[...], bias_ref[...], count, per_group)
    for part in range(2):
        clear_pads(pad_ref.at[part], width)
    pair_weights(kernel_ref, pair_ref)
    stores = []

    def ready(pair):
        for copy in copies[pair]:
            copy.wait()
        if pair >= 1:
            x_copies[pair - 1].wait()

    def fill(at):
        keep = outside(edge_ref, at, rows)

        def temporal(low, high):
            a = half_silu(mine_ext[at, low:high], *mine_factors).astype(BF16)
            b = half_silu(other_ext[at, low:high], *other_factors).astype(BF16)
            value = jnp.dot(jnp.concatenate([a, b], axis=1), temporal_ref[...], preferred_element_type=F32)
            return value if keep is None else value * keep

        spread_row(temporal, width, channels, pad_ref.at[at % 2], taps_ref, at)

    def drain(pair, part):
        half = width // 2
        low = part * half
        result = pair_dot(taps_ref, 2 * pair, pair_ref, low, low + half)
        for out in range(2):
            row = 2 * pair + out
            video = x_ext[row, low : low + half].astype(F32)
            predicted = (video + result[:, out * channels : (out + 1) * channels]) * (1.0 / math.sqrt(2.0))
            pred_made[row, low : low + half] = predicted
            next_made[row, low : low + half] = (plan_ref[0] * video + plan_ref[1] * predicted).astype(BF16)
        if part == 1:
            band = pl.ds(2 * pair, 2)
            for made, ref, sem in ((pred_made, pred_ref, pred_sem), (next_made, next_ref, next_sem)):
                stores.append(pltpu.make_async_copy(made.at[band], ref.at[band], sem.at[pair]))
                stores[-1].start()

    staggered(rows // 2 + 1, ready, fill, drain)
    for store in stores:
        store.wait()


def final(edge, plan, first, outer, other, other_outer, x, sums, other_sums, gain, bias, mixing, kernel, count, per_group):
    rows, width, channels = x.shape
    depth = 3 * channels
    anywhere = pl.BlockSpec(memory_space=pl.ANY)
    return pl.pallas_call(
        functools.partial(final_kernel, count, per_group),
        in_specs=[
            pl.BlockSpec(memory_space=pltpu.SMEM),
            pl.BlockSpec(memory_space=pltpu.SMEM),
            anywhere,
            anywhere,
            anywhere,
            anywhere,
            anywhere,
            whole(16, channels),
            whole(16, channels),
            whole(1, channels),
            whole(1, channels),
            whole(2 * channels, channels),
            whole(3, depth, channels),
        ],
        out_specs=[anywhere, anywhere],
        out_shape=[
            jax.ShapeDtypeStruct((rows, width, channels), BF16),
            jax.ShapeDtypeStruct((rows, width, channels), F32),
        ],
        scratch_shapes=[
            pltpu.VMEM((rows + 2, width, channels), BF16),
            pltpu.VMEM((rows + 2, width, channels), BF16),
            pltpu.VMEM((rows, width, channels), BF16),
            pltpu.VMEM((rows, width, channels), BF16),
            pltpu.VMEM((rows, width, channels), F32),
            pltpu.VMEM((2, width + 2 * PAD, channels), F32),
            pltpu.VMEM((rows + 2, width, depth), BF16),
            pltpu.VMEM((4 * depth, 2 * channels), BF16),
            pltpu.SemaphoreType.DMA((rows + 2,)),
            pltpu.SemaphoreType.DMA((rows + 2,)),
            pltpu.SemaphoreType.DMA((rows // 2,)),
            pltpu.SemaphoreType.DMA((rows // 2,)),
            pltpu.SemaphoreType.DMA((rows // 2,)),
        ],
        compiler_params=pltpu.CompilerParams(vmem_limit_bytes=VMEM_LIMIT),
        cost_estimate=pl.CostEstimate(flops=24 * rows * width * channels * channels, bytes_accessed=12 * rows * width * channels, transcendentals=2 * rows * width * channels),
        name="final",
    )(edge, plan, first, outer, other, other_outer, x, sums, other_sums, gain, bias, mixing, kernel)


def body(noisy_video, timestep, embed_weight, norm_gain, norm_bias, conv_first, temporal_weight, conv_second):
    frames, rows, width, channels = noisy_video.shape
    bands = lax.axis_size("rows")
    assert frames == 1 and lax.axis_size("frames") == 2
    assert rows % 2 == 0 and bands & (bands - 1) == 0
    per_group = channels // GROUPS
    count = rows * bands * width * per_group
    x = noisy_video[0]
    band = lax.axis_index("rows")
    frame = lax.axis_index("frames")
    edge = jnp.stack([band > 0, band < bands - 1]).astype(jnp.int32)

    forward = [(i, i + 1) for i in range(bands - 1)]
    backward = [(b, a) for a, b in forward]
    swap = [(0, 1), (1, 0)]

    def all_bands(value):
        reach = 1
        while reach < bands:
            value = value + lax.ppermute(value, "rows", [(i, i ^ reach) for i in range(bands)])
            reach *= 2
        return value

    low_b = lax.ppermute(x[rows - 1 :], "rows", forward)
    high_a = lax.ppermute(x[:1], "rows", backward)
    low_a = lax.ppermute(x[rows - 2 : rows - 1], "rows", forward)
    high_b = lax.ppermute(x[1:2], "rows", backward)

    step_now = timestep[0]
    film = embed_time(step_now, embed_weight)
    signal_now, noise_now = signal_noise(step_now)
    signal_prev, noise_prev = signal_noise(step_now - STRIDE)
    ratio = signal_prev / signal_now
    plan = jnp.stack([ratio, noise_prev - ratio * noise_now])

    sums_one = all_bands(moments(x))
    gain_one, bias_one = norm_gain[0:1], norm_bias[0:1]
    kernel_one = conv_first.reshape(3, 3 * channels, channels)
    first, partial = conv_one(
        x, low_b, high_a, edge, sums_one, gain_one, bias_one, film, kernel_one, count, per_group
    )
    other = lax.ppermute(first, "frames", swap)
    outer = outer_rows(
        x, low_a, low_b, high_a, high_b, sums_one, gain_one, bias_one, film, kernel_one, count, per_group
    )
    other_outer = lax.ppermute(outer, "frames", swap)
    sums_two = all_bands(partial)
    other_two = lax.ppermute(sums_two, "frames", swap)
    side = jnp.where(frame == 0, temporal_weight[2], temporal_weight[0])
    mixing = jnp.concatenate([temporal_weight[1], side], axis=0)

    depth = 3 * channels
    next_video, predicted = final(
        edge, plan, first, outer, other, other_outer, x, sums_two, other_two,
        norm_gain[1:2], norm_bias[1:2], mixing, conv_second.reshape(3, depth, channels), count, per_group,
    )
    return next_video[None], predicted[None]


def solution(mesh):
    image = P(("clips", "frames"), "rows", None, None)
    return jax.shard_map(
        body,
        mesh=mesh,
        in_specs=(image, P("clips"), P(), P(), P(), P(), P(), P()),
        out_specs=(image, image),
        check_vma=False,
    )
```

```python
import functools
import math

import jax
import jax.numpy as jnp
from jax import lax
from jax.experimental import pallas as pl
from jax.experimental.pallas import tpu as pltpu
from jax.sharding import PartitionSpec as P


GROUPS = 32
TSTEPS = 1000
STRIDE = 8
PAD = 8
CHUNK = 128
F32 = jnp.float32
BF16 = jnp.bfloat16
MIB = 1024 * 1024


def signal_noise(step_value):
    frac = (step_value.astype(F32) / TSTEPS + 0.008) / 1.008
    level = jnp.cos(frac * (math.pi / 2)) ** 2
    return (jnp.sqrt(level), jnp.sqrt(1.0 - level))


def embed_time(step_value, embed_weight):
    half = embed_weight.shape[0] // 2
    freqs = jnp.exp(-math.log(10000.0) * jnp.arange(half, dtype=F32) / half)
    angles = step_value.astype(F32) * freqs
    feats = jnp.concatenate([jnp.sin(angles), jnp.cos(angles)]).astype(BF16)
    return jnp.dot(feats[None, :], embed_weight, preferred_element_type=F32)


def fold(values):
    _, channels = values.shape
    wide = jnp.sum(values.reshape(-1, 64, channels), axis=0)
    return jnp.sum(wide.reshape(-1, 8, channels), axis=0)


def moments_kernel(x_ref, out_ref, ext_ref, sem):
    rows, width, channels = x_ref.shape
    copies = [pltpu.make_async_copy(x_ref.at[row], ext_ref.at[row], sem.at[row]) for row in range(rows)]
    for copy in copies:
        copy.start()
    out_ref[...] = jnp.zeros_like(out_ref)
    for row in range(rows):
        copies[row].wait()

        def chunk(at, sums):
            low = pl.multiple_of(at * CHUNK, CHUNK)
            values = ext_ref[row, pl.ds(low, CHUNK)].astype(F32).reshape(-1, 32, channels)
            first, second = sums
            for piece in range(values.shape[0]):
                first = first + values[piece]
                second = second + values[piece] * values[piece]
            return first, second

        zero = jnp.zeros((32, channels), F32)
        first, second = lax.fori_loop(0, width // CHUNK, chunk, (zero, zero), unroll=2)
        out_ref[0:8] += jnp.sum(first.reshape(-1, 8, channels), axis=0)
        out_ref[8:16] += jnp.sum(second.reshape(-1, 8, channels), axis=0)


def moments(x):
    rows, _, channels = x.shape
    return pl.pallas_call(
        moments_kernel,
        in_specs=[pl.BlockSpec(memory_space=pl.ANY)],
        out_specs=pl.BlockSpec(memory_space=pltpu.VMEM),
        out_shape=jax.ShapeDtypeStruct((16, channels), F32),
        scratch_shapes=[pltpu.VMEM(x.shape, BF16), pltpu.SemaphoreType.DMA((rows,))],
        compiler_params=pltpu.CompilerParams(vmem_limit_bytes=8 * MIB),
        cost_estimate=pl.CostEstimate(flops=3 * x.size, bytes_accessed=2 * x.size, transcendentals=0),
        name="moments",
    )(x)


def half_factors(sums, gain, bias, count, per_group):
    first = jnp.sum(sums[0:8], axis=0, keepdims=True)
    second = jnp.sum(sums[8:16], axis=0, keepdims=True)
    both = jnp.concatenate([first, second] * 4, axis=0)
    channels = both.shape[1]
    lane = lax.broadcasted_iota(jnp.int32, both.shape, 1)
    total, reach = both, 1
    while reach < per_group:
        up = pltpu.roll(total, channels - reach, 1)
        down = pltpu.roll(total, reach, 1)
        total = total + jnp.where((lane // reach) % 2 == 0, up, down)
        reach *= 2
    mean = total[0:1] / count
    inverse = lax.rsqrt(total[1:2] / count - mean * mean + 1e-05)
    scale = inverse * gain
    return 0.5 * scale, 0.5 * (bias - mean * scale)


def half_silu(value, scale, offset):
    half = value.astype(F32) * scale + offset
    return half + half * jnp.tanh(half)


def spread_row(source, width, channels, pad_ref, taps_ref, at):
    for low in range(0, width, CHUNK):
        value = source(low, low + CHUNK)
        pad_ref[PAD + low : PAD + low + CHUNK] = value
        taps_ref[at, low : low + CHUNK, channels : 2 * channels] = value.astype(BF16)
    for low in range(0, width, CHUNK):
        for tap in (0, 2):
            start = PAD + low + tap - 1
            taps_ref[at, low : low + CHUNK, tap * channels : (tap + 1) * channels] = pad_ref[
                start : start + CHUNK
            ].astype(BF16)


def clear_pads(pad_ref, width):
    for low in (0, PAD + width):
        pad_ref[low : low + PAD] = jnp.zeros((PAD, pad_ref.shape[1]), F32)


def pair_weights(kernel_ref, pair_ref):
    depth, channels = kernel_ref.shape[1:]
    for row in range(4):
        for out in range(2):
            block = pair_ref.at[row * depth : (row + 1) * depth, out * channels : (out + 1) * channels]
            if 0 <= row - out <= 2:
                block[...] = kernel_ref[row - out]
            else:
                block[...] = jnp.zeros((depth, channels), BF16)


def pair_dot(taps_ref, first, pair_ref, low, high):
    left = jnp.concatenate([taps_ref[first + row, low:high] for row in range(4)], axis=1)
    return jnp.dot(left, pair_ref[...], preferred_element_type=F32)


def start_rows(flag_ref, low_refs, x_ref, high_refs, ext_ref, sem):
    rows = x_ref.shape[0]
    for frame in range(2):

        @pl.when(flag_ref[2] == frame)
        def _(frame=frame):
            pltpu.make_async_copy(low_refs[frame], ext_ref.at[0], sem.at[0]).start()
            pltpu.make_async_copy(high_refs[frame], ext_ref.at[rows + 1], sem.at[rows + 1]).start()

    sources = [low_refs[0]] + [x_ref.at[row] for row in range(rows)] + [high_refs[0]]
    copies = [pltpu.make_async_copy(ref, ext_ref.at[at], sem.at[at]) for at, ref in enumerate(sources)]
    for copy in copies[1:-1]:
        copy.start()
    return [copies[at : at + 2] for at in range(0, rows + 2, 2)]


def sums_of(flag_ref, sums_ref, other):
    second, first = sums_ref[0:16], sums_ref[16:32]
    is_second = (flag_ref[2] == 1) != other
    return jnp.where(is_second, second, first)


def staggered(pairs, ready, fill, drain):
    for step in range(pairs + 1):
        if step < pairs:
            ready(step)
        for part in range(2):
            if step < pairs:
                fill(2 * step + part)
            if step >= 2:
                drain(step - 2, part)


def conv_one_kernel(
    count, per_group, edge_ref, low_ref, x_ref, high_ref, relay_ref, sums_ref, gain_ref, bias_ref,
    film_ref, kernel_ref, out_ref, stats_ref, ext_ref, made_ref, pad_ref, taps_ref, pair_ref, sem, out_sem,
):
    rows, width, channels = x_ref.shape
    lows, highs = (low_ref.at[0], relay_ref.at[0]), (high_ref.at[0], relay_ref.at[1])
    copies = start_rows(edge_ref, lows, x_ref, highs, ext_ref, sem)
    scale, offset = half_factors(sums_of(edge_ref, sums_ref, False), gain_ref[...], bias_ref[...], count, per_group)
    gain = 1.0 + film_ref[0:1, :channels]
    shift = film_ref[0:1, channels:]
    for part in range(2):
        clear_pads(pad_ref.at[part], width)
    pair_weights(kernel_ref, pair_ref)
    stats_ref[...] = jnp.zeros_like(stats_ref)
    stores = []

    def ready(pair):
        for copy in copies[pair]:
            copy.wait()

    def fill(at):
        keep = outside(edge_ref, at, rows)

        def activated(low, high):
            value = half_silu(ext_ref[at, low:high], scale, offset)
            return value if keep is None else value * keep

        spread_row(activated, width, channels, pad_ref.at[at % 2], taps_ref, at)

    def drain(pair, part):
        half = width // 2
        low = part * half
        result = pair_dot(taps_ref, 2 * pair, pair_ref, low, low + half)
        first = second = 0.0
        for out in range(2):
            value = result[:, out * channels : (out + 1) * channels] * gain + shift
            made_ref[2 * pair + out, low : low + half] = value.astype(BF16)
            first += fold(value)
            second += fold(value * value)
        stats_ref[0:8] += first
        stats_ref[8:16] += second
        if part == 1:
            band = pl.ds(2 * pair, 2)
            stores.append(pltpu.make_async_copy(made_ref.at[band], out_ref.at[band], out_sem.at[pair]))
            stores[-1].start()

    staggered(rows // 2 + 1, ready, fill, drain)
    for store in stores:
        store.wait()


def outside(edge_ref, at, rows):
    if at == 0:
        return edge_ref[0].astype(F32)
    return edge_ref[1].astype(F32) if at == rows + 1 else None


def whole(*shape):
    return pl.BlockSpec(shape, lambda *_: (0,) * len(shape))


def conv_one(x, low, high, relay, edge, sums, gain, bias, film, kernel, count, per_group):
    rows, width, channels = x.shape
    depth = 3 * channels
    anywhere = pl.BlockSpec(memory_space=pl.ANY)
    return pl.pallas_call(
        functools.partial(conv_one_kernel, count, per_group),
        in_specs=[
            pl.BlockSpec(memory_space=pltpu.SMEM),
            anywhere,
            anywhere,
            anywhere,
            anywhere,
            whole(32, channels),
            whole(1, channels),
            whole(1, channels),
            whole(1, 2 * channels),
            whole(3, depth, channels),
        ],
        out_specs=[anywhere, whole(16, channels)],
        out_shape=[
            jax.ShapeDtypeStruct((rows, width, channels), BF16),
            jax.ShapeDtypeStruct((16, channels), F32),
        ],
        scratch_shapes=[
            pltpu.VMEM((rows + 2, width, channels), BF16),
            pltpu.VMEM((rows, width, channels), BF16),
            pltpu.VMEM((2, width + 2 * PAD, channels), F32),
            pltpu.VMEM((rows + 2, width, depth), BF16),
            pltpu.VMEM((4 * depth, 2 * channels), BF16),
            pltpu.SemaphoreType.DMA((rows + 2,)),
            pltpu.SemaphoreType.DMA((rows // 2,)),
        ],
        compiler_params=pltpu.CompilerParams(vmem_limit_bytes=20 * MIB),
        cost_estimate=pl.CostEstimate(flops=18 * rows * width * channels * channels, bytes_accessed=4 * rows * width * channels, transcendentals=rows * width * channels),
        name="conv_one",
    )(edge, low, x, high, relay, sums, gain, bias, film, kernel)


def outer_rows_kernel(
    count, per_group, edge_ref, low_a, low_b, high_a, high_b, x_ref, x_other, sums_ref, gain_ref, bias_ref,
    film_ref, kernel_ref, out_ref, ext_ref, made_ref, pad_ref, taps_ref, weight_ref, sem, out_sem,
):
    rows, width, channels = x_ref.shape
    held = x_other.shape[0]

    @pl.when(edge_ref[2] == 0)
    def _():
        copies = [pltpu.make_async_copy(kernel_ref, weight_ref, sem.at[12])]
        for frame in range(2):
            x_low = (x_ref.at[0], x_other.at[0])[frame]
            x_high = (x_ref.at[rows - 1], x_other.at[held - 1])[frame]
            sources = (low_a.at[frame], low_b.at[frame], x_low, x_high, high_a.at[frame], high_b.at[frame])
            for side, ref in enumerate(sources):
                at = 6 * frame + side
                copies.append(pltpu.make_async_copy(ref, ext_ref.at[at], sem.at[at]))
        for copy in copies:
            copy.start()
        for part in range(2):
            clear_pads(pad_ref.at[part], width)
        gain = 1.0 + film_ref[0:1, :channels]
        shift = film_ref[0:1, channels:]
        for copy in copies:
            copy.wait()
        weights = weight_ref[...].reshape(-1, channels)

        def row(at, carry):
            sums = jnp.where(at >= 2, sums_ref[0:16], sums_ref[16:32])
            scale, offset = half_factors(sums, gain_ref[...], bias_ref[...], count, per_group)
            for part in range(3):
                spread_row(
                    lambda low, high: half_silu(ext_ref[3 * at + part, low:high], scale, offset),
                    width, channels, pad_ref.at[part % 2], taps_ref, part,
                )
            for low in range(0, width, width // 2):
                high = low + width // 2
                left = jnp.concatenate([taps_ref[part, low:high] for part in range(3)], axis=1)
                result = jnp.dot(left, weights, preferred_element_type=F32)
                made_ref[at, low:high] = (result * gain + shift).astype(BF16)
            return carry

        lax.fori_loop(0, 4, row, 0)
        store = pltpu.make_async_copy(made_ref, out_ref, out_sem)
        store.start()
        store.wait()


def outer_rows(x, x_other, low_a, low_b, high_a, high_b, edge, sums, gain, bias, film, kernel, count, per_group):
    _, width, channels = x.shape
    depth = 3 * channels
    anywhere = pl.BlockSpec(memory_space=pl.ANY)
    return pl.pallas_call(
        functools.partial(outer_rows_kernel, count, per_group),
        in_specs=[
            pl.BlockSpec(memory_space=pltpu.SMEM),
            anywhere,
            anywhere,
            anywhere,
            anywhere,
            anywhere,
            anywhere,
            pl.BlockSpec(memory_space=pltpu.VMEM),
            pl.BlockSpec(memory_space=pltpu.VMEM),
            pl.BlockSpec(memory_space=pltpu.VMEM),
            pl.BlockSpec(memory_space=pltpu.VMEM),
            anywhere,
        ],
        out_specs=anywhere,
        out_shape=jax.ShapeDtypeStruct((4, width, channels), BF16),
        scratch_shapes=[
            pltpu.VMEM((12, width, channels), BF16),
            pltpu.VMEM((4, width, channels), BF16),
            pltpu.VMEM((2, width + 2 * PAD, channels), F32),
            pltpu.VMEM((3, width, depth), BF16),
            pltpu.VMEM((3, depth, channels), BF16),
            pltpu.SemaphoreType.DMA((13,)),
            pltpu.SemaphoreType.DMA,
        ],
        compiler_params=pltpu.CompilerParams(vmem_limit_bytes=20 * MIB),
        cost_estimate=pl.CostEstimate(flops=72 * width * channels * channels, bytes_accessed=32 * width * channels, transcendentals=12 * width * channels),
        name="outer_rows",
    )(edge, low_a, low_b, high_a, high_b, x, x_other, sums, gain, bias, film, kernel)


def final_kernel(
    count, per_group, edge_ref, plan_ref, mine_ref, other_ref, made_outer, sent_outer,
    x_ref, sums_ref, gain_ref, bias_ref, temporal_ref, kernel_ref,
    next_ref, pred_ref, mine_ext, other_ext, x_ext, next_made, pred_made, pad_ref, taps_ref, pair_ref,
    mine_sem, other_sem, x_sem, next_sem, pred_sem,
):
    rows, width, channels = mine_ref.shape
    mine_copies = start_rows(
        edge_ref, (made_outer.at[0], sent_outer.at[2]), mine_ref, (made_outer.at[1], sent_outer.at[3]), mine_ext, mine_sem
    )
    other_copies = start_rows(
        edge_ref, (made_outer.at[2], sent_outer.at[0]), other_ref, (made_outer.at[3], sent_outer.at[1]), other_ext, other_sem
    )
    copies = [a + b for a, b in zip(mine_copies, other_copies)]
    x_copies = []
    for pair in range(rows // 2):
        band = pl.ds(2 * pair, 2)
        x_copies.append(pltpu.make_async_copy(x_ref.at[band], x_ext.at[band], x_sem.at[pair]))
        x_copies[-1].start()
    mine_factors, other_factors = (
        half_factors(sums_of(edge_ref, sums_ref, other), gain_ref[...], bias_ref[...], count, per_group)
        for other in (False, True)
    )
    for part in range(2):
        clear_pads(pad_ref.at[part], width)
    pair_weights(kernel_ref, pair_ref)
    stores = []

    def ready(pair):
        for copy in copies[pair]:
            copy.wait()
        if pair >= 1:
            x_copies[pair - 1].wait()

    def fill(at):
        keep = outside(edge_ref, at, rows)

        def temporal(low, high):
            a = half_silu(mine_ext[at, low:high], *mine_factors).astype(BF16)
            b = half_silu(other_ext[at, low:high], *other_factors).astype(BF16)
            value = jnp.dot(jnp.concatenate([a, b], axis=1), temporal_ref[...], preferred_element_type=F32)
            return value if keep is None else value * keep

        spread_row(temporal, width, channels, pad_ref.at[at % 2], taps_ref, at)

    def drain(pair, part):
        half = width // 2
        low = part * half
        result = pair_dot(taps_ref, 2 * pair, pair_ref, low, low + half)
        for out in range(2):
            row = 2 * pair + out
            video = x_ext[row, low : low + half].astype(F32)
            predicted = (video + result[:, out * channels : (out + 1) * channels]) * (1.0 / math.sqrt(2.0))
            pred_made[row, low : low + half] = predicted
            next_made[row, low : low + half] = (plan_ref[0] * video + plan_ref[1] * predicted).astype(BF16)
        if part == 1:
            band = pl.ds(2 * pair, 2)
            for made, ref, sem in ((pred_made, pred_ref, pred_sem), (next_made, next_ref, next_sem)):
                stores.append(pltpu.make_async_copy(made.at[band], ref.at[band], sem.at[pair]))
                stores[-1].start()

    staggered(rows // 2 + 1, ready, fill, drain)
    for store in stores:
        store.wait()


def final(edge, plan, first, other, outer, sent_outer, x, sums, gain, bias, mixing, kernel, count, per_group):
    rows, width, channels = x.shape
    depth = 3 * channels
    anywhere = pl.BlockSpec(memory_space=pl.ANY)
    return pl.pallas_call(
        functools.partial(final_kernel, count, per_group),
        in_specs=[
            pl.BlockSpec(memory_space=pltpu.SMEM),
            pl.BlockSpec(memory_space=pltpu.SMEM),
            anywhere,
            anywhere,
            anywhere,
            anywhere,
            anywhere,
            whole(32, channels),
            whole(1, channels),
            whole(1, channels),
            whole(2 * channels, channels),
            whole(3, depth, channels),
        ],
        out_specs=[anywhere, anywhere],
        out_shape=[
            jax.ShapeDtypeStruct((rows, width, channels), BF16),
            jax.ShapeDtypeStruct((rows, width, channels), F32),
        ],
        scratch_shapes=[
            pltpu.VMEM((rows + 2, width, channels), BF16),
            pltpu.VMEM((rows + 2, width, channels), BF16),
            pltpu.VMEM((rows, width, channels), BF16),
            pltpu.VMEM((rows, width, channels), BF16),
            pltpu.VMEM((rows, width, channels), F32),
            pltpu.VMEM((2, width + 2 * PAD, channels), F32),
            pltpu.VMEM((rows + 2, width, depth), BF16),
            pltpu.VMEM((4 * depth, 2 * channels), BF16),
            pltpu.SemaphoreType.DMA((rows + 2,)),
            pltpu.SemaphoreType.DMA((rows + 2,)),
            pltpu.SemaphoreType.DMA((rows // 2,)),
            pltpu.SemaphoreType.DMA((rows // 2,)),
            pltpu.SemaphoreType.DMA((rows // 2,)),
        ],
        compiler_params=pltpu.CompilerParams(vmem_limit_bytes=32 * MIB),
        cost_estimate=pl.CostEstimate(flops=24 * rows * width * channels * channels, bytes_accessed=12 * rows * width * channels, transcendentals=2 * rows * width * channels),
        name="final",
    )(edge, plan, first, other, outer, sent_outer, x, sums, gain, bias, mixing, kernel)


def send(value, pairs):
    bands = lax.axis_size("rows")
    flat = [(a * bands + b, c * bands + d) for (a, b), (c, d) in pairs]
    return lax.ppermute(value, ("frames", "rows"), flat)


def block(noisy_video, timestep, embed_weight, norm_gain, norm_bias, conv_first, temporal_weight, conv_second):
    frames, rows, width, channels = noisy_video.shape
    bands = lax.axis_size("rows")
    assert frames == 1 and lax.axis_size("frames") == 2
    assert rows % 2 == 0 and bands & (bands - 1) == 0
    per_group = channels // GROUPS
    depth = 3 * channels
    count = rows * bands * width * per_group
    x = noisy_video[0]
    band = lax.axis_index("rows")
    frame = lax.axis_index("frames")
    edge = jnp.stack([band > 0, band < bands - 1, frame > 0]).astype(jnp.int32)

    every = range(bands)
    up = [((0, b), (1, b)) for b in every]
    down = [((1, b), (0, b)) for b in every]
    forward = [((0, b), (0, b + 1)) for b in every if b + 1 < bands]
    backward = [(target, source) for source, target in forward]

    def all_bands(value):
        total = jnp.concatenate([value, send(value, up)], axis=0)
        reach = 1
        while reach < bands:
            total = total + send(total, [((1, b), (1, b ^ reach)) for b in every])
            reach *= 2
        back = send(total, down)
        return jnp.where(frame == 0, back, total)

    x_other = send(jnp.concatenate([x[:2], x[rows - 2 :]], axis=0), down)
    low_b = send(jnp.stack([x[rows - 1], x_other[3]]), forward)
    high_a = send(jnp.stack([x[0], x_other[0]]), backward)
    low_a = send(jnp.stack([x[rows - 2], x_other[2]]), forward)
    high_b = send(jnp.stack([x[1], x_other[1]]), backward)

    step_now = timestep[0]
    film = embed_time(step_now, embed_weight)
    signal_now, noise_now = signal_noise(step_now)
    signal_prev, noise_prev = signal_noise(step_now - STRIDE)
    ratio = signal_prev / signal_now
    plan = jnp.stack([ratio, noise_prev - ratio * noise_now])

    sums_one = all_bands(moments(x))
    gain_one, bias_one = norm_gain[0:1], norm_bias[0:1]
    kernel_one = conv_first.reshape(3, depth, channels)
    relay = send(jnp.stack([low_b[1], high_a[1]]), up)
    first, partial = conv_one(
        x, low_b, high_a, relay, edge, sums_one, gain_one, bias_one, film, kernel_one, count, per_group
    )
    other = send(first, up + down)
    sums_two = all_bands(partial)
    outer = outer_rows(
        x, x_other, low_a, low_b, high_a, high_b, edge, sums_one, gain_one, bias_one, film, kernel_one,
        count, per_group,
    )
    sent_outer = send(outer, up)
    side = jnp.where(frame == 0, temporal_weight[2], temporal_weight[0])
    mixing = jnp.concatenate([temporal_weight[1], side], axis=0)
    next_video, predicted = final(
        edge, plan, first, other, outer, sent_outer, x, sums_two, norm_gain[1:2], norm_bias[1:2], mixing,
        conv_second.reshape(3, depth, channels), count, per_group,
    )
    return next_video[None], predicted[None]


def solution(mesh):
    image = P(("clips", "frames"), "rows", None, None)
    return jax.shard_map(
        block,
        mesh=mesh,
        in_specs=(image, P("clips"), P(), P(), P(), P(), P(), P()),
        out_specs=(image, image),
        check_vma=False,
    )
```

```python
import functools
import math

import jax
import jax.numpy as jnp
from jax import lax
from jax.experimental import pallas as pl
from jax.experimental.pallas import tpu as pltpu
from jax.sharding import PartitionSpec as P


GROUPS = 32
TSTEPS = 1000
STRIDE = 8
PAD = 8
CHUNK = 128
F32 = jnp.float32
BF16 = jnp.bfloat16
MIB = 1024 * 1024


def signal_noise(step_value):
    frac = (step_value.astype(F32) / TSTEPS + 0.008) / 1.008
    level = jnp.cos(frac * (math.pi / 2)) ** 2
    return (jnp.sqrt(level), jnp.sqrt(1.0 - level))


def embed_time(step_value, embed_weight):
    half = embed_weight.shape[0] // 2
    freqs = jnp.exp(-math.log(10000.0) * jnp.arange(half, dtype=F32) / half)
    angles = step_value.astype(F32) * freqs
    feats = jnp.concatenate([jnp.sin(angles), jnp.cos(angles)]).astype(BF16)
    return jnp.dot(feats[None, :], embed_weight, preferred_element_type=F32)


def fold(values):
    _, channels = values.shape
    wide = jnp.sum(values.reshape(-1, 64, channels), axis=0)
    return jnp.sum(wide.reshape(-1, 8, channels), axis=0)


def start_edges(flag_ref, band_ref, near_ref, far_ref, sem):
    last = band_ref.shape[0] - 1
    for odd in range(2):

        @pl.when(flag_ref[2] == odd)
        def _(odd=odd):
            rows = (0, last) if odd else (last, 0)
            for at, ref in enumerate((near_ref, far_ref)):
                pltpu.make_async_copy(band_ref.at[rows[at]], ref.at[0], sem.at[at]).start()

    return [pltpu.make_async_copy(band_ref.at[0], ref.at[0], sem.at[at]) for at, ref in enumerate((near_ref, far_ref))]


def moments_kernel(flag_ref, x_ref, out_ref, near_ref, far_ref, ext_ref, sem, edge_sem):
    rows, width, channels = x_ref.shape
    copies = [pltpu.make_async_copy(x_ref.at[row], ext_ref.at[row], sem.at[row]) for row in range(rows)]
    order = [0, rows - 1] + list(range(1, rows - 1))
    for row in order:
        copies[row].start()
    out_ref[...] = jnp.zeros_like(out_ref)
    for row in order[:2]:
        copies[row].wait()
    edges = start_edges(flag_ref, ext_ref, near_ref, far_ref, edge_sem)
    for row in order:
        if row not in order[:2]:
            copies[row].wait()

        def chunk(at, sums):
            low = pl.multiple_of(at * CHUNK, CHUNK)
            values = ext_ref[row, pl.ds(low, CHUNK)].astype(F32).reshape(-1, 32, channels)
            first, second = sums
            for piece in range(values.shape[0]):
                first = first + values[piece]
                second = second + values[piece] * values[piece]
            return first, second

        zero = jnp.zeros((32, channels), F32)
        first, second = lax.fori_loop(0, width // CHUNK, chunk, (zero, zero), unroll=2)
        out_ref[0:8] += jnp.sum(first.reshape(-1, 8, channels), axis=0)
        out_ref[8:16] += jnp.sum(second.reshape(-1, 8, channels), axis=0)
    for copy in edges:
        copy.wait()


def moments(x, edge):
    rows, width, channels = x.shape
    anywhere = pl.BlockSpec(memory_space=pl.ANY)
    row = jax.ShapeDtypeStruct((1, width, channels), BF16)
    return pl.pallas_call(
        moments_kernel,
        in_specs=[pl.BlockSpec(memory_space=pltpu.SMEM), anywhere],
        out_specs=[pl.BlockSpec(memory_space=pltpu.VMEM), anywhere, anywhere],
        out_shape=[jax.ShapeDtypeStruct((16, channels), F32), row, row],
        scratch_shapes=[pltpu.VMEM(x.shape, BF16), pltpu.SemaphoreType.DMA((rows,)), pltpu.SemaphoreType.DMA((2,))],
        compiler_params=pltpu.CompilerParams(vmem_limit_bytes=8 * MIB),
        cost_estimate=pl.CostEstimate(flops=3 * x.size, bytes_accessed=2 * x.size, transcendentals=0),
        name="moments",
    )(edge, x)


def half_factors(sums, gain, bias, count, per_group):
    first = jnp.sum(sums[0:8], axis=0, keepdims=True)
    second = jnp.sum(sums[8:16], axis=0, keepdims=True)
    both = jnp.concatenate([first, second] * 4, axis=0)
    channels = both.shape[1]
    lane = lax.broadcasted_iota(jnp.int32, both.shape, 1)
    total, reach = both, 1
    while reach < per_group:
        up = pltpu.roll(total, channels - reach, 1)
        down = pltpu.roll(total, reach, 1)
        total = total + jnp.where((lane // reach) % 2 == 0, up, down)
        reach *= 2
    mean = total[0:1] / count
    inverse = lax.rsqrt(total[1:2] / count - mean * mean + 1e-05)
    scale = inverse * gain
    return 0.5 * scale, 0.5 * (bias - mean * scale)


def half_silu(value, scale, offset):
    half = value.astype(F32) * scale + offset
    return half + half * jnp.tanh(half)


def spread_row(source, width, channels, pad_ref, taps_ref, at):
    for low in range(0, width, CHUNK):
        value = source(low, low + CHUNK)
        pad_ref[PAD + low : PAD + low + CHUNK] = value
        taps_ref[at, low : low + CHUNK, channels : 2 * channels] = value.astype(BF16)
    for low in range(0, width, CHUNK):
        for tap in (0, 2):
            start = PAD + low + tap - 1
            taps_ref[at, low : low + CHUNK, tap * channels : (tap + 1) * channels] = pad_ref[
                start : start + CHUNK
            ].astype(BF16)


def clear_pads(pad_ref, width):
    for low in (0, PAD + width):
        pad_ref[low : low + PAD] = jnp.zeros((PAD, pad_ref.shape[1]), F32)


def pair_weights(kernel_ref, pair_ref):
    depth, channels = kernel_ref.shape[1:]
    for row in range(4):
        for out in range(2):
            block = pair_ref.at[row * depth : (row + 1) * depth, out * channels : (out + 1) * channels]
            if 0 <= row - out <= 2:
                block[...] = kernel_ref[row - out]
            else:
                block[...] = jnp.zeros((depth, channels), BF16)


def pair_dot(taps_ref, first, pair_ref, low, high):
    left = jnp.concatenate([taps_ref[first + row, low:high] for row in range(4)], axis=1)
    return jnp.dot(left, pair_ref[...], preferred_element_type=F32)


def start_rows(flag_ref, near_ref, x_ref, far_ref, ext_ref, sem):
    rows = x_ref.shape[0]
    for odd in range(2):

        @pl.when(flag_ref[2] == odd)
        def _(odd=odd):
            low, high = (near_ref, far_ref) if odd else (far_ref, near_ref)
            pltpu.make_async_copy(low.at[0], ext_ref.at[0], sem.at[0]).start()
            pltpu.make_async_copy(high.at[0], ext_ref.at[rows + 1], sem.at[rows + 1]).start()

    sources = [near_ref.at[0]] + [x_ref.at[row] for row in range(rows)] + [far_ref.at[0]]
    copies = [pltpu.make_async_copy(ref, ext_ref.at[at], sem.at[at]) for at, ref in enumerate(sources)]
    for copy in copies[1:-1]:
        copy.start()
    return [copies[at : at + 2] for at in range(0, rows + 2, 2)]


def staggered(pairs, ready, fill, drain):
    for step in range(pairs + 1):
        if step < pairs:
            ready(step)
        for part in range(2):
            if step < pairs:
                fill(2 * step + part)
            if step >= 2:
                drain(step - 2, part)


def conv_one_kernel(
    count, per_group, edge_ref, near_ref, x_ref, far_ref, sums_ref, gain_ref, bias_ref,
    film_ref, kernel_ref, out_ref, stats_ref, near_out, far_out, ext_ref, made_ref, pad_ref, taps_ref, pair_ref,
    sem, out_sem, edge_sem,
):
    rows, width, channels = x_ref.shape
    copies = start_rows(edge_ref, near_ref, x_ref, far_ref, ext_ref, sem)
    scale, offset = half_factors(sums_ref[...], gain_ref[...], bias_ref[...], count, per_group)
    gain = 1.0 + film_ref[0:1, :channels]
    shift = film_ref[0:1, channels:]
    for part in range(2):
        clear_pads(pad_ref.at[part], width)
    pair_weights(kernel_ref, pair_ref)
    stats_ref[...] = jnp.zeros_like(stats_ref)
    stores = []

    def ready(pair):
        for copy in copies[pair]:
            copy.wait()

    def fill(at):
        keep = outside(edge_ref, at, rows)

        def activated(low, high):
            value = half_silu(ext_ref[at, low:high], scale, offset)
            return value if keep is None else value * keep

        spread_row(activated, width, channels, pad_ref.at[at % 2], taps_ref, at)

    def drain(pair, part):
        half = width // 2
        low = part * half
        result = pair_dot(taps_ref, 2 * pair, pair_ref, low, low + half)
        first = second = 0.0
        for out in range(2):
            value = result[:, out * channels : (out + 1) * channels] * gain + shift
            made_ref[2 * pair + out, low : low + half] = value.astype(BF16)
            first += fold(value)
            second += fold(value * value)
        stats_ref[0:8] += first
        stats_ref[8:16] += second
        if part == 1:
            band = pl.ds(2 * pair, 2)
            stores.append(pltpu.make_async_copy(made_ref.at[band], out_ref.at[band], out_sem.at[pair]))
            stores[-1].start()

    staggered(rows // 2 + 1, ready, fill, drain)
    stores += start_edges(edge_ref, made_ref, near_out, far_out, edge_sem)
    for store in stores:
        store.wait()


def outside(edge_ref, at, rows):
    if at == 0:
        return edge_ref[0].astype(F32)
    return edge_ref[1].astype(F32) if at == rows + 1 else None


def whole(*shape):
    return pl.BlockSpec(shape, lambda *_: (0,) * len(shape))


def conv_one(x, near, far, edge, sums, gain, bias, film, kernel, count, per_group):
    rows, width, channels = x.shape
    depth = 3 * channels
    anywhere = pl.BlockSpec(memory_space=pl.ANY)
    return pl.pallas_call(
        functools.partial(conv_one_kernel, count, per_group),
        in_specs=[
            pl.BlockSpec(memory_space=pltpu.SMEM),
            anywhere,
            anywhere,
            anywhere,
            whole(16, channels),
            whole(1, channels),
            whole(1, channels),
            whole(1, 2 * channels),
            whole(3, depth, channels),
        ],
        out_specs=[anywhere, whole(16, channels), anywhere, anywhere],
        out_shape=[
            jax.ShapeDtypeStruct((rows, width, channels), BF16),
            jax.ShapeDtypeStruct((16, channels), F32),
            jax.ShapeDtypeStruct((1, width, channels), BF16),
            jax.ShapeDtypeStruct((1, width, channels), BF16),
        ],
        scratch_shapes=[
            pltpu.VMEM((rows + 2, width, channels), BF16),
            pltpu.VMEM((rows, width, channels), BF16),
            pltpu.VMEM((2, width + 2 * PAD, channels), F32),
            pltpu.VMEM((rows + 2, width, depth), BF16),
            pltpu.VMEM((4 * depth, 2 * channels), BF16),
            pltpu.SemaphoreType.DMA((rows + 2,)),
            pltpu.SemaphoreType.DMA((rows // 2,)),
            pltpu.SemaphoreType.DMA((2,)),
        ],
        compiler_params=pltpu.CompilerParams(vmem_limit_bytes=20 * MIB),
        cost_estimate=pl.CostEstimate(flops=18 * rows * width * channels * channels, bytes_accessed=4 * rows * width * channels, transcendentals=rows * width * channels),
        name="conv_one",
    )(edge, near, x, far, sums, gain, bias, film, kernel)


def final_kernel(
    count, per_group, edge_ref, plan_ref, mine_ref, mine_near, mine_far, other_ref, other_near, other_far,
    x_ref, sums_ref, gain_ref, bias_ref, temporal_ref, kernel_ref,
    next_ref, pred_ref, mine_ext, other_ext, x_ext, next_made, pred_made, pad_ref, taps_ref, pair_ref,
    mine_sem, other_sem, x_sem, next_sem, pred_sem,
):
    rows, width, channels = mine_ref.shape
    mine_copies = start_rows(edge_ref, mine_near, mine_ref, mine_far, mine_ext, mine_sem)
    other_copies = start_rows(edge_ref, other_near, other_ref, other_far, other_ext, other_sem)
    copies = [a + b for a, b in zip(mine_copies, other_copies)]
    x_copies = []
    for pair in range(rows // 2):
        band = pl.ds(2 * pair, 2)
        x_copies.append(pltpu.make_async_copy(x_ref.at[band], x_ext.at[band], x_sem.at[pair]))
        x_copies[-1].start()
    mine_factors, other_factors = (
        half_factors(sums_ref[at : at + 16], gain_ref[...], bias_ref[...], count, per_group)
        for at in (0, 16)
    )
    for part in range(2):
        clear_pads(pad_ref.at[part], width)
    pair_weights(kernel_ref, pair_ref)
    stores = []

    def ready(pair):
        for copy in copies[pair]:
            copy.wait()
        if pair >= 1:
            x_copies[pair - 1].wait()

    def fill(at):
        keep = outside(edge_ref, at, rows)

        def temporal(low, high):
            a = half_silu(mine_ext[at, low:high], *mine_factors).astype(BF16)
            b = half_silu(other_ext[at, low:high], *other_factors).astype(BF16)
            value = jnp.dot(jnp.concatenate([a, b], axis=1), temporal_ref[...], preferred_element_type=F32)
            return value if keep is None else value * keep

        spread_row(temporal, width, channels, pad_ref.at[at % 2], taps_ref, at)

    def drain(pair, part):
        half = width // 2
        low = part * half
        result = pair_dot(taps_ref, 2 * pair, pair_ref, low, low + half)
        for out in range(2):
            row = 2 * pair + out
            video = x_ext[row, low : low + half].astype(F32)
            predicted = (video + result[:, out * channels : (out + 1) * channels]) * (1.0 / math.sqrt(2.0))
            pred_made[row, low : low + half] = predicted
            next_made[row, low : low + half] = (plan_ref[0] * video + plan_ref[1] * predicted).astype(BF16)
        if part == 1:
            band = pl.ds(2 * pair, 2)
            for made, ref, sem in ((pred_made, pred_ref, pred_sem), (next_made, next_ref, next_sem)):
                stores.append(pltpu.make_async_copy(made.at[band], ref.at[band], sem.at[pair]))
                stores[-1].start()

    staggered(rows // 2 + 1, ready, fill, drain)
    for store in stores:
        store.wait()


def final(edge, plan, first, near, far, other, other_near, other_far, x, sums, gain, bias, mixing, kernel, count, per_group):
    rows, width, channels = x.shape
    depth = 3 * channels
    anywhere = pl.BlockSpec(memory_space=pl.ANY)
    return pl.pallas_call(
        functools.partial(final_kernel, count, per_group),
        in_specs=[
            pl.BlockSpec(memory_space=pltpu.SMEM),
            pl.BlockSpec(memory_space=pltpu.SMEM),
            anywhere,
            anywhere,
            anywhere,
            anywhere,
            anywhere,
            anywhere,
            anywhere,
            whole(32, channels),
            whole(1, channels),
            whole(1, channels),
            whole(2 * channels, channels),
            whole(3, depth, channels),
        ],
        out_specs=[anywhere, anywhere],
        out_shape=[
            jax.ShapeDtypeStruct((rows, width, channels), BF16),
            jax.ShapeDtypeStruct((rows, width, channels), F32),
        ],
        scratch_shapes=[
            pltpu.VMEM((rows + 2, width, channels), BF16),
            pltpu.VMEM((rows + 2, width, channels), BF16),
            pltpu.VMEM((rows, width, channels), BF16),
            pltpu.VMEM((rows, width, channels), BF16),
            pltpu.VMEM((rows, width, channels), F32),
            pltpu.VMEM((2, width + 2 * PAD, channels), F32),
            pltpu.VMEM((rows + 2, width, depth), BF16),
            pltpu.VMEM((4 * depth, 2 * channels), BF16),
            pltpu.SemaphoreType.DMA((rows + 2,)),
            pltpu.SemaphoreType.DMA((rows + 2,)),
            pltpu.SemaphoreType.DMA((rows // 2,)),
            pltpu.SemaphoreType.DMA((rows // 2,)),
            pltpu.SemaphoreType.DMA((rows // 2,)),
        ],
        compiler_params=pltpu.CompilerParams(vmem_limit_bytes=32 * MIB),
        cost_estimate=pl.CostEstimate(flops=24 * rows * width * channels * channels, bytes_accessed=12 * rows * width * channels, transcendentals=2 * rows * width * channels),
        name="final",
    )(edge, plan, first, near, far, other, other_near, other_far, x, sums, gain, bias, mixing, kernel)


def send(value, pairs):
    bands = lax.axis_size("rows")
    flat = [(a * bands + b, c * bands + d) for (a, b), (c, d) in pairs]
    return lax.ppermute(value, ("frames", "rows"), flat)


def block(noisy_video, timestep, embed_weight, norm_gain, norm_bias, conv_first, temporal_weight, conv_second):
    frames, rows, width, channels = noisy_video.shape
    bands = lax.axis_size("rows")
    assert frames == 1 and lax.axis_size("frames") == 2
    assert rows % 2 == 0 and bands & (bands - 1) == 0
    per_group = channels // GROUPS
    depth = 3 * channels
    count = rows * bands * width * per_group
    x = noisy_video[0]
    band = lax.axis_index("rows")
    frame = lax.axis_index("frames")
    edge = jnp.stack([band > 0, band < bands - 1, band % 2 > 0]).astype(jnp.int32)
    both = range(2)
    every = range(bands)

    def across(reach, turn=0):
        return [((f, b), (f ^ turn, b ^ reach)) for f in both for b in every]

    between = [(b, b + 1) for b in every if b % 2 and b + 1 < bands]
    between = [((f, a), (f, b)) for f in both for pair in between for a, b in (pair, pair[::-1])]

    sums_one, near_edge, far_edge = moments(x, edge)
    sums_one = sums_one + send(sums_one, across(1))
    near = send(near_edge, across(1))
    far = send(far_edge, between)
    reach = 2
    while reach < bands:
        sums_one = sums_one + send(sums_one, across(reach))
        reach *= 2

    step_now = timestep[0]
    film = embed_time(step_now, embed_weight)
    signal_now, noise_now = signal_noise(step_now)
    signal_prev, noise_prev = signal_noise(step_now - STRIDE)
    ratio = signal_prev / signal_now
    plan = jnp.stack([ratio, noise_prev - ratio * noise_now])

    first, partial, near_edge, far_edge = conv_one(
        x, near, far, edge, sums_one, norm_gain[0:1], norm_bias[0:1], film, conv_first.reshape(3, depth, channels),
        count, per_group,
    )
    mine = partial + send(partial, across(1))
    theirs = send(partial, across(0, 1)) + send(partial, across(1, 1))
    sums_two = jnp.concatenate([mine, theirs], axis=0)
    other = send(first, across(0, 1))
    near = send(near_edge, across(1))
    far = send(far_edge, between)
    reach = 2
    while reach < bands:
        sums_two = sums_two + send(sums_two, across(reach))
        reach *= 2
    other_near = send(near, across(0, 1))
    other_far = send(far, across(0, 1))
    side = jnp.where(frame == 0, temporal_weight[2], temporal_weight[0])
    mixing = jnp.concatenate([temporal_weight[1], side], axis=0)
    next_video, predicted = final(
        edge, plan, first, near, far, other, other_near, other_far, x, sums_two, norm_gain[1:2], norm_bias[1:2],
        mixing, conv_second.reshape(3, depth, channels), count, per_group,
    )
    return next_video[None], predicted[None]


def solution(mesh):
    image = P(("clips", "frames"), "rows", None, None)
    return jax.shard_map(
        block,
        mesh=mesh,
        in_specs=(image, P("clips"), P(), P(), P(), P(), P(), P()),
        out_specs=(image, image),
        check_vma=False,
    )
```
